32 devices in a mesh: batch: 2 (over y), seq: 16 (over z, x, core).
Axes of the slice: x: 2, y: 2, z: 4, core: 2. Of those that a mesh axis runs over, the one named last changes fastest.
Arguments:
- inputs: bfloat16 [2, 2, 1024, 768], P(None, 'batch', 'seq'), may hold values from -6 to 6
- params: bfloat16 [7087104], P(('batch', 'seq')), may hold values from -3 to 3, as said below
- segment_ids: int32 [2, 2, 1024], P(None, 'batch'), may hold values from 0 to 15, never falling along the last dimension, each value on 1 to 512 neighbouring positions
- cotangent: bfloat16 [2, 2, 1024, 768], P(None, 'batch', 'seq'), may hold values from -6 to 6
Outputs:
- outputs: bfloat16 [2, 2, 1024, 768], P(None, 'batch', 'seq')
- input_grad: bfloat16 [2, 2, 1024, 768], P(None, 'batch', 'seq')
- param_grad: float32 [7087104], P(('batch', 'seq'))
The draws below stay inside these ranges and needn't reach their ends.
Inputs may be any that keep to these rules, and one draw needn't show every extreme that they name: params holds one after another, each matrix row by row and applied as x times the matrix: w_query, w_key, w_value, w_out (768 x 768 each), w_in (768 x 3072), w_down (3072 x 768), b_query, b_value, b_out, gain_one, shift_one (768 each), b_in (3072), b_down, gain_two, shift_two (768 each). `segment_ids`: ids never fall along a sequence; a document has 1 to 512 tokens.
All inputs are finite; a program needn't handle non-finite values.
Results may differ from the reference program's by a relative error of at most 0.013.
Values may be sent and summed in bfloat16 or wider, within the bound.
No kernel may reach another device: no remote copies, remote signals or barrier semaphores. Data moves between devices by JAX's collectives and lax.ppermute only.
A program may use at most 320 MiB of HBM per device.

```python
import math
import jax
import jax.numpy as jnp
import numpy as np
from jax import lax

D = 768
HEADS = 12
HD = 64
FF = 3072
MICRO = 2
DOCS = 16
SEQS = 2
LENGTH = 1024
PARAMS = 7087104


def draw_params(key, part):
    layout = [(D * D, 1.2 * D ** (-0.5), 0.0), (D * D, 1.2 * D ** (-0.5), 0.0), (D * D, D ** (-0.5), 0.0), (D * D, 4.0 * D ** (-0.5), 0.0), (D * FF, D ** (-0.5), 0.0), (FF * D, 1.4 * FF ** (-0.5), 0.0), (D, 0.5, 0.0), (D, 0.5, 0.0), (D, 0.3, 0.0), (D, 0.15, 1.0), (D, 0.3, 0.0), (FF, 0.5, 0.0), (D, 0.3, 0.0), (D, 0.15, 1.0), (D, 0.3, 0.0)]
    pieces_list = []
    for number, (entry_count, spread, centre) in enumerate(layout):
        subkey = jax.random.fold_in(key, number + 11)
        piece = jax.random.normal(subkey, (entry_count,), jnp.float32) * spread
        pieces_list.append(jnp.clip(centre + piece, -3.0, 3.0))
    return jnp.concatenate(pieces_list).astype(jnp.bfloat16)


def block_levels(own_key, shape, pieces, least, top_value):
    def one(axis_at, shards_of):
        draws = jax.random.uniform(jax.random.fold_in(jax.random.fold_in(own_key, 6), axis_at), (shards_of,), jnp.float32, least / len(pieces), top_value / len(pieces))
        return jnp.repeat(jnp.exp(draws), shape[axis_at] // shards_of).reshape((-1,) + (1,) * (len(shape) - axis_at - 1))

    factor_of = one(*pieces[0])
    for cut in pieces[1:]:
        factor_of = factor_of * one(*cut)
    return factor_of


def length_profile(count, total, limit, slope):
    loads = [(1 << 20) // math.isqrt(standing ** slope) + 1 for standing in range(2, count + 1)]
    rest, holding = total - limit - (count - 1), [1] * (count - 1)
    while rest > 0:
        candidates = [i for i in range(count - 1) if holding[i] < limit]
        pool, budget = sum([loads[i] for i in candidates]), rest
        for i in candidates:
            addition = min(limit - holding[i], max(1, budget * loads[i] // pool), rest)
            holding[i] = holding[i] + addition
            rest = rest - addition
    return np.array([limit] + holding)


def ragged_sizes(rng, number_of, total, reach, lean):
    if number_of == 2:
        one = jax.random.randint(rng, (), max(1, total - reach), min(reach, total - 1) + 1)
        return jnp.stack([one, total - one])
    sizes = jnp.asarray(length_profile(number_of, total, reach, lean), jnp.int32)
    pairs = (number_of - 1) // 2
    donor, taker = sizes[1:1 + 2 * pairs:2], sizes[2:2 + 2 * pairs:2]
    slack = jnp.minimum(donor - 1, reach - taker)
    moved = jax.random.randint(jax.random.fold_in(rng, 1), (pairs,), 0, 1 << 20) % (slack + 1)
    sizes = sizes.at[1:1 + 2 * pairs:2].set(donor - moved).at[2:2 + 2 * pairs:2].set(taker + moved)
    return sizes[jax.random.permutation(jax.random.fold_in(rng, 2), number_of)]


def normal_values(key, dims, scale, most, pieces=(), dtype=jnp.bfloat16):
    array = jax.random.normal(key, dims, jnp.float32) * scale
    if len(pieces) > 0:
        array = block_levels(key, dims, pieces, -0.22, 0.18) * array
    return jnp.clip(array, min=-most, max=most).astype(dtype)


def setup_inputs(seed: int = 0) -> dict:
    key_of = jax.random.split(jax.random.key(seed), 5)
    inputs = normal_values(key_of[0], (MICRO, SEQS, LENGTH, D), 1.0, 6.0, ((1, 2), (2, 16)))
    params = draw_params(jax.random.fold_in(key_of[4], 71), 0)
    segment_ids = jax.vmap(lambda own: jnp.searchsorted(jnp.cumsum(ragged_sizes(own, DOCS, LENGTH, LENGTH // 2, 2)), jnp.arange(LENGTH), side="right"))(jax.random.split(key_of[2], MICRO * SEQS)).reshape((MICRO, SEQS, LENGTH)).astype(jnp.int32)
    cotangent = normal_values(key_of[3], (MICRO, SEQS, LENGTH, D), 1.0, 6.0, ((1, 2), (2, 16)))
    return {"inputs": inputs, "params": params, "segment_ids": segment_ids, "cotangent": cotangent}


@jax.custom_vjp
def low(v):
    return lax.optimization_barrier(v.astype(jnp.bfloat16)).astype(jnp.float32)

@jax.custom_vjp
def low_back(v):
    return v

def low_keep(v):
    return (low(v), None)

def low_pass(kept, grad):
    return (grad,)

def back_keep(v):
    return (v, None)

def back_low(kept, grad):
    return (low(grad),)
low.defvjp(low_keep, low_pass)
low_back.defvjp(back_keep, back_low)
epsilon = 1e-12
highest = lax.Precision.HIGHEST

def unpack_params(flat_params):
    layout = [(D, D), (D, D), (D, D), (D, D), (D, FF), (FF, D), (D,), (D,), (D,), (D,), (D,), (FF,), (D,), (D,), (D,)]
    pieces_list = []
    offset = 0
    for extent in layout:
        entry_count = math.prod(extent)
        pieces_list.append(flat_params[offset:offset + entry_count].reshape(extent))
        offset += entry_count
    return pieces_list

def layer_norm(values_in, gain_vec, shift_vec):
    average = lax.optimization_barrier(jnp.mean(values_in, axis=-1, keepdims=True))
    centred = values_in - average
    variance = lax.optimization_barrier(jnp.mean(centred * centred, axis=-1, keepdims=True))
    return centred * lax.rsqrt(variance + epsilon) * gain_vec + shift_vec

def matmul_high(left_side, right_side):
    return jnp.dot(left_side, right_side, precision=highest)

def layer(inputs_seq, flat_params, segment_row):
    w_query, w_key, w_value, w_out, w_in, w_down, b_query, b_value, b_out, gain_one, shift_one, b_in, b_down, gain_two, shift_two = unpack_params(flat_params)
    query = low_back(low(matmul_high(inputs_seq, w_query) + b_query))
    keys = low_back(low(matmul_high(inputs_seq, w_key)))
    values = low_back(low(matmul_high(inputs_seq, w_value) + b_value))
    same_doc = segment_row[:, None] == segment_row[None, :]
    scale = HD ** (-0.5)

    def split_heads(matrix):
        return matrix.reshape(LENGTH, HEADS, HD).transpose(1, 0, 2)

    def attend_head(operands):
        query_head, key_head, value_head = operands
        scores = low_back(jnp.dot(query_head, key_head.T, precision=highest) * scale)
        masked = jnp.where(same_doc, scores, -1e+30)
        probability = low(jax.nn.softmax(masked, axis=-1))
        return jnp.dot(probability, value_head, precision=highest)
    mixture = lax.map(jax.checkpoint(attend_head), (split_heads(query), split_heads(keys), split_heads(values)))
    attended = low_back(low(mixture.transpose(1, 0, 2).reshape(LENGTH, D)))
    branch = low_back(matmul_high(attended, w_out) + b_out)
    first_norm = layer_norm(inputs_seq + branch, gain_one, shift_one)
    inner_act = low_back(matmul_high(low(first_norm), w_in) + b_in)
    hidden = low(jax.nn.gelu(inner_act, approximate=False))
    second = low_back(matmul_high(hidden, w_down) + b_down)
    return layer_norm(first_norm + second, gain_two, shift_two)

def reference(inputs, params, segment_ids, cotangent):
    flat_params = params.astype(jnp.float32)
    seq_count = MICRO * SEQS
    inputs_rows = inputs.reshape(seq_count, LENGTH, D)
    cotangent_rows = cotangent.reshape(seq_count, LENGTH, D)
    segment_rows = segment_ids.reshape(seq_count, LENGTH)

    def accumulate(grad_total, operands):
        inputs_seq, cotangent_seq, segment_row = operands
        outputs_seq, pull_back = jax.vjp(lambda values_in, weights_in: layer(values_in, weights_in, segment_row), inputs_seq.astype(jnp.float32), flat_params)
        d_inputs, d_params = pull_back(cotangent_seq.astype(jnp.float32))
        return (grad_total + d_params, (outputs_seq.astype(jnp.bfloat16), d_inputs.astype(jnp.bfloat16)))
    grad_total, (outputs, input_grad) = lax.scan(accumulate, jnp.zeros((PARAMS,), jnp.float32), (inputs_rows, cotangent_rows, segment_rows))
    return (outputs.reshape(MICRO, SEQS, LENGTH, D), input_grad.reshape(MICRO, SEQS, LENGTH, D), grad_total)
```

```python
import math
from functools import partial

import jax
import jax.numpy as jnp
from jax import lax
from jax.experimental import pallas as pl
from jax.experimental.pallas import tpu as pltpu
from jax.sharding import PartitionSpec as P

D = 768
HD = 64
FF = 3072
HEADS = 12
GROUP = 4
GW = GROUP * HD
AUX = 128
TILE = 16
epsilon = 1e-12
ALL = ("batch", "seq")
f32 = jnp.float32
bf16 = jnp.bfloat16
NEG = -1e30


def project(a, b):
    return jnp.dot(a, b, preferred_element_type=f32)


def outer_product(a, b):
    return lax.dot_general(a, b, (((0,), (0,)), ((), ())), preferred_element_type=f32)


def backward_product(a, b):
    return lax.dot_general(a, b, (((1,), (1,)), ((), ())), preferred_element_type=f32)


def stack_heads(block):
    lane = lax.broadcasted_iota(jnp.int32, block.shape, 1) // HD
    zero = jnp.zeros_like(block)
    return jnp.concatenate([jnp.where(lane == h, block, zero) for h in range(GROUP)], axis=0)


def unstack_heads(stacked, rows):
    lane = lax.broadcasted_iota(jnp.int32, (rows, GW), 1) // HD
    total = stacked[:rows]
    for h in range(1, GROUP):
        total = jnp.where(lane == h, stacked[h * rows : (h + 1) * rows], total)
    return total


def flat_rows(ref):
    value = ref[...]
    return value.reshape(-1, value.shape[-1])


def nt(a, b):
    return lax.dot_general(a, b, (((1,), (1,)), ((), ())), preferred_element_type=f32)


def forward_kernel(q_ref, k_ref, v_ref, sq_ref, sk_ref, o_ref, aux_ref):
    group = pl.program_id(1)
    q = q_ref[0]
    rows = q.shape[0]
    keys, values = flat_rows(k_ref), flat_rows(v_ref)
    same = sq_ref[0] == sk_ref[0]
    scores = nt(stack_heads(q), keys) * (HD**-0.5)
    lane = lax.broadcasted_iota(jnp.int32, (rows, AUX), 1)
    probs, aux = [], jnp.zeros((rows, AUX), f32)
    for h in range(GROUP):
        masked = jnp.where(same, scores[h * rows : (h + 1) * rows], NEG)
        top = jnp.max(masked, axis=1, keepdims=True)
        weight = jnp.exp(masked - top)
        total = jnp.sum(weight, axis=1, keepdims=True)
        probs.append((weight / total).astype(bf16))
        head = group * GROUP + h
        aux = aux + jnp.where((lane % 32 == head) & (lane < 96), top + jnp.log(total), 0.0)
    mixed = jnp.dot(jnp.concatenate(probs, axis=0), values, preferred_element_type=f32)
    o_ref[0] = unstack_heads(mixed, rows)

    @pl.when(group == 0)
    def _():
        aux_ref[0] = aux

    @pl.when(group > 0)
    def _():
        aux_ref[0] = aux_ref[0] + aux


def pack_kernel(da_ref, o_ref, aux_ref, out_ref):
    da = da_ref[...].astype(bf16)
    prod = da.astype(f32) * o_ref[...]
    head = lax.broadcasted_iota(jnp.int32, (D, AUX), 0) // HD
    lane_c = lax.broadcasted_iota(jnp.int32, (D, AUX), 1)
    select = jnp.where((lane_c % 32 == head + HEADS) & (lane_c < 96), 1.0, 0.0).astype(f32)
    delta = jnp.dot(prod, select, precision=lax.Precision.HIGHEST, preferred_element_type=f32)
    both = aux_ref[...] + delta
    lane = lax.broadcasted_iota(jnp.int32, both.shape, 1)
    high = both.astype(bf16).astype(f32)
    rest = both - high
    middle = rest.astype(bf16).astype(f32)
    low = rest - middle
    out_ref[:, :D] = da
    out_ref[:, D:] = jnp.where(lane < 32, high, jnp.where(lane < 64, middle, low)).astype(bf16)


def query_grad_kernel(q_ref, k_ref, v_ref, da_ref, sq_ref, sk_ref, dq_ref):
    q = q_ref[0]
    rows = q.shape[0]
    keys, values = flat_rows(k_ref), flat_rows(v_ref)
    same = sq_ref[0] == sk_ref[0]
    scores = nt(stack_heads(q), keys) * (HD**-0.5)
    d_prob = nt(stack_heads(da_ref[0]), values)
    parts = []
    for h in range(GROUP):
        masked = jnp.where(same, scores[h * rows : (h + 1) * rows], NEG)
        weight = jnp.exp(masked - jnp.max(masked, axis=1, keepdims=True))
        prob = weight / jnp.sum(weight, axis=1, keepdims=True)
        dp = d_prob[h * rows : (h + 1) * rows]
        delta = jnp.sum(prob * dp, axis=1, keepdims=True)
        parts.append((prob * (dp - delta)).astype(bf16))
    mixed = jnp.dot(jnp.concatenate(parts, axis=0), keys, preferred_element_type=f32)
    dq_ref[0] = (unstack_heads(mixed, rows) * (HD**-0.5)).astype(bf16)


def key_grad_kernel(k_ref, v_ref, q_ref, da_ref, aux_ref, sk_ref, sq_ref, dk_ref, dv_ref):
    group = pl.program_id(1)
    k = k_ref[0]
    rows = k.shape[0]
    queries, d_att, aux = flat_rows(q_ref), flat_rows(da_ref), flat_rows(aux_ref)
    same = sk_ref[0] == sq_ref[0]
    row = lax.broadcasted_iota(jnp.int32, (2 * GROUP, AUX), 0)
    lane = lax.broadcasted_iota(jnp.int32, (2 * GROUP, AUX), 1)
    wanted = group * GROUP + row % GROUP + HEADS * (row // GROUP)
    select = jnp.where((lane % 32 == wanted) & (lane < 96), 1.0, 0.0).astype(bf16)
    stats = nt(select, aux)
    scores = nt(stack_heads(k), queries) * (HD**-0.5)
    d_prob = nt(stack_heads(v_ref[0]), d_att)
    probs, parts = [], []
    for h in range(GROUP):
        masked = jnp.where(same, scores[h * rows : (h + 1) * rows], NEG)
        prob = jnp.exp(masked - stats[h : h + 1])
        dp = d_prob[h * rows : (h + 1) * rows]
        probs.append(prob.astype(bf16))
        parts.append((prob * (dp - stats[GROUP + h : GROUP + h + 1])).astype(bf16))
    d_key = jnp.dot(jnp.concatenate(parts, axis=0), queries, preferred_element_type=f32)
    d_value = jnp.dot(jnp.concatenate(probs, axis=0), d_att, preferred_element_type=f32)
    dk_ref[0] = (unstack_heads(d_key, rows) * (HD**-0.5)).astype(bf16)
    dv_ref[0] = unstack_heads(d_value, rows).astype(bf16)


def own_spec(rows):
    return pl.BlockSpec((1, rows, GW), lambda m, g: (m, 0, g))


def all_spec(count, rows):
    return pl.BlockSpec((count, None, rows, GW), lambda m, g: (0, m, 0, g))


def column_spec(rows):
    return pl.BlockSpec((1, rows, 1), lambda m, g: (m, 0, 0))


def row_spec(length):
    return pl.BlockSpec((1, 1, length), lambda m, g: (m, 0, 0))


def attention_forward(q, k, v, seg_own, seg_all):
    micro, rows, _ = q.shape
    count, length = k.shape[0], seg_all.shape[-1]
    cost = pl.CostEstimate(
        flops=2 * micro * 3 * 2 * GW * length * GW,
        bytes_accessed=4 * k.size,
        transcendentals=micro * HEADS * rows * length,
    )
    return pl.pallas_call(
        forward_kernel,
        grid=(micro, D // GW),
        in_specs=[
            own_spec(rows),
            all_spec(count, rows),
            all_spec(count, rows),
            column_spec(rows),
            row_spec(length),
        ],
        out_specs=[own_spec(rows), pl.BlockSpec((1, rows, AUX), lambda m, g: (m, 0, 0))],
        out_shape=[
            jax.ShapeDtypeStruct((micro, rows, D), f32),
            jax.ShapeDtypeStruct((micro, rows, AUX), f32),
        ],
        cost_estimate=cost,
        name="attend",
    )(q, k, v, seg_own, seg_all)


def pack_gradient(d_att, mixed, aux):
    return pl.pallas_call(
        pack_kernel,
        out_shape=jax.ShapeDtypeStruct((d_att.shape[0], D + AUX), bf16),
        name="pack",
    )(d_att, mixed, aux)


def attention_query_grad(q, k, v, packed, seg_own, seg_all):
    micro, rows, _ = q.shape
    count, length = k.shape[0], seg_all.shape[-1]
    cost = pl.CostEstimate(
        flops=3 * micro * 3 * 2 * GW * length * GW,
        bytes_accessed=4 * k.size,
        transcendentals=micro * HEADS * rows * length,
    )
    return pl.pallas_call(
        query_grad_kernel,
        grid=(micro, D // GW),
        in_specs=[
            own_spec(rows),
            all_spec(count, rows),
            all_spec(count, rows),
            own_spec(rows),
            column_spec(rows),
            row_spec(length),
        ],
        out_specs=own_spec(rows),
        out_shape=jax.ShapeDtypeStruct((micro, rows, D), bf16),
        cost_estimate=cost,
        name="query_grad",
    )(q, k, v, packed, seg_own, seg_all)


def attention_key_grad(k, v, q, packed, seg_own, seg_all):
    micro, rows, _ = k.shape
    count, length = q.shape[0], seg_all.shape[-1]
    cost = pl.CostEstimate(
        flops=4 * micro * 3 * 2 * GW * length * GW,
        bytes_accessed=4 * q.size,
        transcendentals=micro * HEADS * rows * length,
    )
    return pl.pallas_call(
        key_grad_kernel,
        grid=(micro, D // GW),
        in_specs=[
            own_spec(rows),
            own_spec(rows),
            all_spec(count, rows),
            all_spec(count, rows),
            pl.BlockSpec((count, None, rows, AUX), lambda m, g: (0, m, 0, D // AUX)),
            column_spec(rows),
            row_spec(length),
        ],
        out_specs=[own_spec(rows), own_spec(rows)],
        out_shape=[jax.ShapeDtypeStruct((micro, rows, D), bf16)] * 2,
        cost_estimate=cost,
        name="key_grad",
    )(k, v, q, packed, packed, seg_own, seg_all)


class Plan:
    def __init__(self, shard, devices):
        total = shard * devices
        assert total % D == 0
        self.shard, self.devices, self.rows = shard, devices, total // D
        self.base = [d * shard // D // TILE * TILE for d in range(devices)]
        ends = [-(-(d + 1) * shard // D) for d in range(devices)]
        need = max(e - b for e, b in zip(ends, self.base))
        self.block = -(-need // TILE) * TILE
        self.offset = [d * shard - b * D for d, b in enumerate(self.base)]

    def place(self, flat, me):
        offset = me * self.shard - me * self.shard // D // TILE * TILE * D
        wide = jnp.zeros((self.block * D,), flat.dtype)
        wide = lax.dynamic_update_slice(wide, flat, (offset,))
        return wide.reshape(self.block, D)

    def take(self, block, me):
        offset = me * self.shard - me * self.shard // D // TILE * TILE * D
        return lax.dynamic_slice(block.reshape(-1), (offset,), (self.shard,))

    def assemble(self, blocks, first, last):
        marks = {first, last}
        for b in self.base:
            for m in (b, b + self.block):
                if first < m < last:
                    marks.add(m)
        marks = sorted(marks)
        pieces = []
        for a, z in zip(marks, marks[1:]):
            parts = [
                blocks[d][a - b : z - b]
                for d, b in enumerate(self.base)
                if b <= a and z <= b + self.block
            ]
            piece = parts[0]
            for part in parts[1:]:
                piece = piece + part
            pieces.append(piece)
        return pieces[0] if len(pieces) == 1 else jnp.concatenate(pieces, axis=0)

    def cut(self, matrices):
        blocks = []
        for b in self.base:
            pieces, at, end = [], 0, b + self.block
            for matrix in matrices:
                rows = matrix.shape[0]
                lo, hi = max(b, at), min(end, at + rows)
                if lo < hi:
                    pieces.append(matrix[lo - at : hi - at])
                at += rows
            if end > at:
                pieces.append(jnp.zeros((end - max(at, b), D), matrices[0].dtype))
            blocks.append(pieces[0] if len(pieces) == 1 else jnp.concatenate(pieces, axis=0))
        return jnp.stack(blocks)


def norm(values):
    average = jnp.mean(values, axis=-1, keepdims=True)
    centred = values - average
    variance = jnp.mean(centred * centred, axis=-1, keepdims=True)
    inverse = lax.rsqrt(variance + epsilon)
    return centred * inverse, inverse


def norm_back(gradient, normed, inverse):
    mean_one = jnp.mean(gradient, axis=-1, keepdims=True)
    mean_two = jnp.mean(gradient * normed, axis=-1, keepdims=True)
    return inverse * (gradient - mean_one - normed * mean_two)


def column_sum(matrix):
    return jnp.sum(matrix.astype(f32), axis=0)


def body(seq_count, batch_count, inputs, params, segment_ids, cotangent):
    micro, _, rows, _ = inputs.shape
    tokens = micro * rows
    plan = Plan(params.shape[0], seq_count * batch_count)
    place_seq = lax.axis_index("seq")
    me = lax.axis_index("batch") * seq_count + place_seq
    length = segment_ids.shape[-1]

    x_own = inputs[:, 0]
    x_flat = x_own.reshape(tokens, D)
    x_all = lax.all_gather(x_own, "seq", axis=0, tiled=False)
    blocks = lax.all_gather(plan.place(params, me), ALL, axis=0, tiled=False)

    def matrix(first, count):
        return plan.assemble(blocks, first, first + count)

    w_query, w_key, w_value, w_out = (matrix(i * D, D) for i in range(4))
    w_in = matrix(4 * D, FF).reshape(D, FF)
    w_down = matrix(4 * D + FF, FF)
    vectors = matrix(4 * D + 2 * FF, 12).astype(f32)
    b_query, b_value, b_out, gain_one, shift_one = (vectors[i] for i in range(5))
    b_in = vectors[5:9].reshape(FF)
    b_down, gain_two, shift_two = (vectors[i] for i in range(9, 12))

    seg = segment_ids[:, 0]
    seg_own = lax.dynamic_slice_in_dim(seg, place_seq * rows, rows, axis=1)[:, :, None]
    seg_all = seg[:, None, :]

    x_rows = x_all.reshape(-1, D)
    split = (seq_count, micro, rows, D)
    q_all = (project(x_rows, w_query) + b_query).astype(bf16).reshape(split)
    k_all = project(x_rows, w_key).astype(bf16).reshape(split)
    v_all = (project(x_rows, w_value) + b_value).astype(bf16).reshape(split)
    q_own, k_own, v_own = (
        lax.dynamic_index_in_dim(a, place_seq, 0, keepdims=False) for a in (q_all, k_all, v_all)
    )

    mixed, aux = attention_forward(q_own, k_all, v_all, seg_own, seg_all)
    mixed = mixed.reshape(tokens, D)
    aux = aux.reshape(tokens, AUX)
    attended = mixed.astype(bf16)
    res_one = x_flat.astype(f32) + project(attended, w_out) + b_out
    n_one, r_one = norm(res_one)
    first_norm = n_one * gain_one + shift_one
    first_low = first_norm.astype(bf16)
    inner = project(first_low, w_in) + b_in
    phi_cdf = 0.5 * (1.0 + lax.erf(inner * math.sqrt(0.5)))
    hidden = (inner * phi_cdf).astype(bf16)
    res_two = first_norm + project(hidden, w_down) + b_down
    n_two, r_two = norm(res_two)
    outputs = (n_two * gain_two + shift_two).astype(bf16)

    grad = cotangent[:, 0].reshape(tokens, D).astype(f32)
    d_gain_two = column_sum(grad * n_two)
    d_shift_two = column_sum(grad)
    d_res_two = norm_back(grad * gain_two, n_two, r_two)
    d_second = d_res_two.astype(bf16)
    slope = phi_cdf + inner * (jnp.exp(-0.5 * inner * inner) * (1.0 / math.sqrt(2.0 * math.pi)))
    d_inner = (backward_product(d_second, w_down) * slope).astype(bf16)
    d_first = d_res_two + backward_product(d_inner, w_in)
    d_gain_one = column_sum(d_first * n_one)
    d_shift_one = column_sum(d_first)
    d_res_one = norm_back(d_first * gain_one, n_one, r_one)
    d_branch = d_res_one.astype(bf16)
    d_att = backward_product(d_branch, w_out)

    packed = pack_gradient(d_att, mixed, aux).reshape(micro, rows, D + AUX)
    packed_all = lax.all_gather(packed, "seq", axis=0, tiled=False)
    d_query = attention_query_grad(q_own, k_all, v_all, packed, seg_own, seg_all)
    d_query = d_query.reshape(tokens, D)
    d_w_down = outer_product(hidden, d_second).astype(bf16)
    d_w_in = outer_product(first_low, d_inner).astype(bf16)
    d_w_out = outer_product(attended, d_branch).astype(bf16)

    d_keys, d_values = attention_key_grad(k_own, v_own, q_all, packed_all, seg_own, seg_all)
    d_keys = d_keys.reshape(tokens, D)
    d_values = d_values.reshape(tokens, D)
    d_w_query = outer_product(x_flat, d_query).astype(bf16)
    d_w_key = outer_product(x_flat, d_keys).astype(bf16)
    d_w_value = outer_product(x_flat, d_values).astype(bf16)
    d_tokens = (
        backward_product(d_query, w_query)
        + backward_product(d_keys, w_key)
        + backward_product(d_values, w_value)
        + d_res_one
    ).astype(bf16)

    d_vectors = jnp.concatenate(
        [
            column_sum(d_query)[None],
            column_sum(d_values)[None],
            column_sum(d_branch)[None],
            d_gain_one[None],
            d_shift_one[None],
            column_sum(d_inner).reshape(4, D),
            column_sum(d_second)[None],
            d_gain_two[None],
            d_shift_two[None],
        ],
        axis=0,
    ).astype(bf16)
    cut = plan.cut(
        [d_w_query, d_w_key, d_w_value, d_w_out, d_w_in.reshape(FF, D), d_w_down, d_vectors]
    )
    mine = lax.psum_scatter(cut, ALL, scatter_dimension=0, tiled=False)
    share = plan.take(mine.astype(f32), me)
    shape = (micro, 1, rows, D)
    return outputs.reshape(shape), d_tokens.reshape(shape), share


def solution(mesh):
    token_spec = P(None, "batch", "seq", None)
    return jax.shard_map(
        partial(body, mesh.shape["seq"], mesh.shape["batch"]),
        mesh=mesh,
        in_specs=(token_spec, P(ALL), P(None, "batch", None), token_spec),
        out_specs=(token_spec, token_spec, P(ALL)),
        check_vma=False,
    )
```
